32 devices in a mesh: tm: 8 (over z, x), space: 4 (over y, core).
Axes of the slice: x: 2, y: 2, z: 4, core: 2. Of those that a mesh axis runs over, the one named last changes fastest.
Arguments:
- frames: bfloat16 [32, 16, 128, 128], P('tm', 'space'), may hold values from -6 to 6
- conv_weight: bfloat16 [3456, 128], replicated, may hold values from -0.109375 to 0.109375
- conv_bias: float32 [128], replicated, may hold values from -3 to 3
- projection: float32 [128, 6], replicated, may hold values from -1 to 1
- levels: int32 [6], replicated, may hold values from 3 to 8, as said below
- centres: int32 [8, 16, 768], P(None, 'space', 'tm'), may hold values from 0 to 7, as said below
- code_grad: float32 [8, 16, 768], P(None, 'space', 'tm'), may hold values from -6 to 6
Outputs:
- quantized: float32 [8, 16, 768], P(None, 'space', 'tm')
- weight_grad: float32 [3456, 128], P('tm', 'space')
- projection_grad: float32 [128, 6], replicated
- bias_grad: float32 [128], replicated
The draws below stay inside these ranges and needn't reach their ends.
Inputs may be any that keep to these rules, and one draw needn't show every extreme that they name: Level counts of the FSQ channels; in every draw some channel has 3 levels and some has 8. centres[g, h, q] is below levels[q % 6].
All inputs are finite; a program needn't handle non-finite values.
Results may differ from the reference program's by a relative error of at most 0.0024.
Values may be sent and summed in bfloat16 or wider, within the bound.
A program may use at most 64 MiB of HBM per device.

```python
import jax
import jax.numpy as jnp
from jax import lax

CH = 128
L = 6
W = 128
F = 32
H = 16
TL = 8
LW = 768
KC = 3456


def level_table(key):
    drawn_base = jax.random.randint(jax.random.fold_in(key, 11), (L,), 3, 9)
    channel_order = jax.random.permutation(jax.random.fold_in(key, 12), L)
    return drawn_base.at[channel_order[0]].set(8).at[channel_order[1]].set(3).astype(jnp.int32)


def draw_levels(key, part):
    return level_table(key)


def draw_centres(key, part):
    column_levels = jnp.tile(level_table(key), W)
    return jax.random.randint(jax.random.fold_in(key, 13), (TL, H, LW), 0, column_levels).astype(jnp.int32)


def level_of(own_key, shape, pieces, smallest, top_value):
    level, own = 1.0, jax.random.fold_in(own_key, 6)
    for position, parts in pieces:
        heights = jnp.exp(jax.random.uniform(jax.random.fold_in(own, position), (parts,), jnp.float32, smallest / len(pieces), top_value / len(pieces)))
        level = level * jnp.repeat(heights, shape[position] // parts).reshape([-1 if axis == position else 1 for axis in range(len(shape))])
    return level


def centred(key, dims, spread, bound, pieces=(), kind=jnp.bfloat16):
    entries = jax.random.normal(key, dims, jnp.float32) * spread
    if len(pieces) > 0:
        entries = level_of(key, dims, pieces, -0.22, 0.18) * entries
    return jnp.clip(entries, min=-bound, max=bound).astype(kind)


def setup_inputs(seed: int = 0) -> dict:
    key_list = jax.random.split(jax.random.key(seed), 8)
    frames = centred(key_list[0], (F, H, W, CH), 1.0, 6.0, ((0, 8), (1, 4)))
    conv_weight = centred(key_list[1], (KC, CH), KC ** -0.5, 0.109375)
    conv_bias = centred(key_list[2], (CH,), 0.5, 3.0, (), jnp.float32)
    projection = centred(key_list[3], (CH, L), (CH // 4) ** -0.5, 1.0, (), jnp.float32)
    levels = draw_levels(jax.random.fold_in(key_list[7], 71), 0)
    centres = draw_centres(jax.random.fold_in(key_list[7], 71), 0)
    code_grad = centred(key_list[6], (TL, H, LW), 1.0, 6.0, ((1, 4), (2, 8)), jnp.float32)
    return {"frames": frames, "conv_weight": conv_weight, "conv_bias": conv_bias, "projection": projection, "levels": levels, "centres": centres, "code_grad": code_grad}


offset_scale = 0.45
commit_weight = 0.25
highest = lax.Precision.HIGHEST


def widen_frames(frame_block):
    frame_width = frame_block.shape[2]
    padded = jnp.pad(frame_block, ((0, 0), (1, 1), (1, 1), (0, 0)))
    return jnp.concatenate([padded[:, :, column_shift:column_shift + frame_width] for column_shift in range(3)], axis=3)


def tap_slabs(widened, frame_count, row_count):
    triple = widened.shape[3]
    slabs = []
    for time_tap in range(3):
        for row_tap in range(3):
            slabs.append(widened[time_tap:time_tap + frame_count, row_tap:row_tap + row_count].reshape(-1, triple))
    return slabs


def reference(frames, conv_weight, conv_bias, projection, levels, centres, code_grad):
    channels = frames.shape[3]
    triple = 3 * channels
    cell_count = H * W
    padded_time = jnp.concatenate([frames[:1], frames[:1], frames], 0)

    def forward(group):
        frame_block = lax.dynamic_slice_in_dim(padded_time, (group * 4).astype(jnp.int32), 6, 0)
        slabs = tap_slabs(widen_frames(frame_block), 4, H)
        preact = jnp.zeros((4 * cell_count, channels), jnp.float32) + conv_bias
        for tap_number in range(9):
            preact = preact + jnp.dot(slabs[tap_number], conv_weight[tap_number * triple:(tap_number + 1) * triple], preferred_element_type=jnp.float32)
        activated = lax.optimization_barrier(jax.nn.silu(preact).astype(jnp.bfloat16))
        pooled = activated.astype(jnp.float32).reshape(4, cell_count, channels).sum(0) * 0.25
        return preact, pooled

    group_index = jnp.arange(TL, dtype=jnp.int32)
    preact_all, pooled_all = lax.map(forward, group_index)
    latent = jnp.dot(pooled_all, projection, precision=highest).reshape(TL, H, LW)
    half_range = (levels.astype(jnp.float32) - 1.0) * 0.5
    half_column = jnp.tile(half_range, W)
    quantized = (centres.astype(jnp.float32) - half_column) / half_column
    squashed = jnp.tanh(latent)
    grad_scale = float(F * H * W) ** -0.5
    code_step = (code_grad / half_column + 2.0 * commit_weight * offset_scale * squashed) * offset_scale * (1.0 - squashed * squashed) * grad_scale
    code_step = code_step.reshape(TL, cell_count, L)
    projection_grad = jnp.einsum("gnc,gnl->cl", pooled_all, code_step, precision=highest)
    pooled_grad = jnp.dot(code_step, projection.T, precision=highest)

    def backward(carry, inputs):
        weight_sum, bias_sum = carry
        preact, grad_group, group = inputs
        frame_block = lax.dynamic_slice_in_dim(padded_time, (group * 4).astype(jnp.int32), 6, 0)
        slabs = tap_slabs(widen_frames(frame_block), 4, H)
        sigmoid_pre = jax.nn.sigmoid(preact)
        silu_slope = sigmoid_pre * (1.0 + preact * (1.0 - sigmoid_pre))
        pre_grad = (0.25 * grad_group[None] * silu_slope.reshape(4, cell_count, channels)).reshape(-1, channels)
        low_grad = pre_grad.astype(jnp.bfloat16)
        blocks = jnp.concatenate([lax.dot_general(tap_slab, low_grad, (((0,), (0,)), ((), ())), preferred_element_type=jnp.float32) for tap_slab in slabs], 0)
        return (weight_sum + blocks, bias_sum + pre_grad.sum(0)), None

    start = (jnp.zeros((27 * channels, channels), jnp.float32), jnp.zeros((channels,), jnp.float32))
    final_carry, unused_out = lax.scan(backward, start, (preact_all, pooled_grad, group_index))
    weight_grad, bias_grad = final_carry
    return quantized, weight_grad, projection_grad, bias_grad
```

```python
import functools

import jax
import jax.numpy as jnp
from jax import lax
from jax.experimental import pallas as pl
from jax.experimental.pallas import tpu as pltpu
from jax.sharding import PartitionSpec as P

offset_scale = 0.45
commit_weight = 0.25
highest = lax.Precision.HIGHEST
MESH = pl.DeviceIdType.MESH
f32, bf16 = jnp.float32, jnp.bfloat16


def dot(a, b, ca, cb, precision=None):
    return lax.dot_general(
        a, b, (((ca,), (cb,)), ((), ())), preferred_element_type=f32, precision=precision
    )


def per_level(levels_ref, index, count):
    half = jnp.ones(index.shape, f32)
    for j in range(count):
        half = jnp.where(index == j, (levels_ref[j].astype(f32) - 1.0) * 0.5, half)
    return half


def block_kernel(
    T, S, scale,
    frames, weight, bias, proj, levels, centres, code_grad,
    quant_out, weight_out, small_out,
    xb, cg_send, cg_recv, pscr, slope_t, gt, acc, stage1, recv1, sum2, stage2, recv2,
    total, own3, stage3, recv3, sm_send, sm_recv, st_send, st_recv,
    local_sem, halo_s, halo_r, cg_s, cg_r, ss_s, ss_r, ts_s, ts_r,
    core_s, core_r, y_s, y_r, tm_s, tm_r,
):
    Y = S // 2
    F, R, W, C = frames.shape
    L = levels.shape[0]
    TILE = code_grad.shape[2]
    oc = C // S
    KC = weight.shape[0]
    KA = KC // 3
    KT = KC // T
    KTP = stage3.shape[2]
    cells = R * W
    t = lax.axis_index("tm")
    s = lax.axis_index("space")
    y, core = s // 2, s % 2
    up_t, dn_t, up_s, dn_s = t < T - 1, t > 0, s < S - 1, s > 0

    barrier = pltpu.get_barrier_semaphore()

    def signal(tt, ss):
        pl.semaphore_signal(barrier, inc=1, device_id=(tt, ss), device_id_type=MESH)

    for d in range(1, S):
        signal(t, lax.rem(s + d, S))
    for d in range(1, T):
        signal(lax.rem(t + d, T), s)
    for ct, dt in ((up_t, 1), (dn_t, -1)):
        for cs_, ds in ((up_s, 1), (dn_s, -1)):
            @pl.when(jnp.logical_and(ct, cs_))
            def _():
                signal(t + dt, s + ds)

    own = pltpu.make_async_copy(frames, xb.at[2 : 2 + F, 1 : 1 + R], local_sem.at[0])
    own.start()
    first = [
        pltpu.make_async_copy(frames.at[0], xb.at[k, 1 : 1 + R], local_sem.at[1 + k])
        for k in range(2)
    ]

    @pl.when(t == 0)
    def _():
        for copy in first:
            copy.start()

    cg_send[...] = jnp.zeros_like(cg_send)
    cg_send[:, 0:R, 0:TILE] = code_grad[...]

    def diag(cond, dt, ds):
        return jnp.where(cond, 1, 0)

    n_t = jnp.where(up_t, 1, 0) + jnp.where(dn_t, 1, 0)
    n_s = jnp.where(up_s, 1, 0) + jnp.where(dn_s, 1, 0)
    pl.semaphore_wait(barrier, (S - 1) + (T - 1) + n_t * n_s)

    def remote(src, dst, ss_, rs_, tt, sp):
        return pltpu.make_async_remote_copy(
            src_ref=src, dst_ref=dst, send_sem=ss_, recv_sem=rs_,
            device_id=(tt, sp), device_id_type=MESH,
        )

    H = R + 1
    halos = [
        (up_s, dn_s, remote(frames.at[:, R - 1], xb.at[2 : 2 + F, 0],
                            halo_s.at[0], halo_r.at[0], t, s + 1)),
        (dn_s, up_s, remote(frames.at[:, 0], xb.at[2 : 2 + F, H],
                            halo_s.at[1], halo_r.at[1], t, s - 1)),
        (up_t, dn_t, remote(frames.at[F - 2 : F], xb.at[0:2, 1:H],
                            halo_s.at[2], halo_r.at[2], t + 1, s)),
        (jnp.logical_and(up_t, up_s), jnp.logical_and(dn_t, dn_s),
         remote(frames.at[F - 2 : F, R - 1], xb.at[0:2, 0],
                halo_s.at[3], halo_r.at[3], t + 1, s + 1)),
        (jnp.logical_and(up_t, dn_s), jnp.logical_and(dn_t, up_s),
         remote(frames.at[F - 2 : F, 0], xb.at[0:2, H],
                halo_s.at[4], halo_r.at[4], t + 1, s - 1)),
    ]

    def start_if(cond, copy):
        @pl.when(cond)
        def _():
            copy.start()

    def recv_if(cond, copy):
        @pl.when(cond)
        def _():
            copy.wait_recv()

    def sent_if(cond, copy):
        @pl.when(cond)
        def _():
            copy.wait_send()

    for sends, _, copy in halos:
        start_if(sends, copy)

    def cg_copy(d):
        to = lax.rem(t + d, T)
        return remote(cg_send.at[to], cg_recv.at[d], cg_s.at[d], cg_r.at[d], to, s)

    for d in range(1, T):
        cg_copy(d).start()

    lane3 = lax.broadcasted_iota(jnp.int32, centres.shape, 2)
    half3 = per_level(levels, lax.rem(lane3, L), L)
    quant_out[...] = (centres[...].astype(f32) - half3) / half3

    pscr[...] = jnp.zeros_like(pscr)
    pscr[:, 0:L] = proj[...]
    proj_t = pscr[...].T[0:8]

    @pl.when(s == 0)
    def _():
        xb[:, 0] = jnp.zeros((F + 2, W, C), bf16)

    @pl.when(s == S - 1)
    def _():
        xb[:, H] = jnp.zeros((F + 2, W, C), bf16)

    row = lax.broadcasted_iota(jnp.int32, (cells, C), 0) % W

    def conv_frame(f):
        slabs = []
        weights = []
        for a in range(3):
            for b in range(3):
                slabs.append(xb[f + a, b : b + R].reshape(cells, C))
                k0 = (a * 3 + b) * 3 * C
                weights.append(
                    jnp.concatenate([weight[k0 + c * C : k0 + (c + 1) * C] for c in range(3)], 1)
                )
        out = dot(jnp.concatenate(slabs, 1), jnp.concatenate(weights, 0), 1, 0)
        left = jnp.where(row == 0, 0.0, pltpu.roll(out[:, 0:C], 1, 0))
        right = jnp.where(row == W - 1, 0.0, pltpu.roll(out[:, 2 * C :], cells - 1, 0))
        pre = out[:, C : 2 * C] + bias[...] + left + right
        sig = 1.0 / (1.0 + jnp.exp(-pre))
        act = (pre * sig).astype(bf16).astype(f32)
        slope = sig * (1.0 + pre * (1.0 - sig))
        for h in range(R):
            slope_t[f * R + h] = slope[h * W : (h + 1) * W].T
        return act

    own.wait()
    for _, gets, copy in halos[:2]:
        recv_if(gets, copy)
    pooled = conv_frame(2) + conv_frame(3)

    for _, gets, copy in halos[2:]:
        recv_if(gets, copy)

    @pl.when(t == 0)
    def _():
        for k in range(2):
            first[k].wait()
            xb[k, 0] = xb[2, 0]
            xb[k, H] = xb[2, H]

    pooled = (pooled + conv_frame(0) + conv_frame(1)) * 0.25

    for d in range(1, T):
        cg_copy(d).wait_recv()
    wt = TILE // L
    mine = cg_send[pl.ds(t, 1)]
    pieces = [mine]
    for d in range(1, T):
        pieces.append(cg_recv[d : d + 1])
    cg_all = jnp.concatenate(pieces, 0).reshape(T * 8, 128)
    r_i = lax.broadcasted_iota(jnp.int32, (T * 8, cells), 0)
    q_i = lax.broadcasted_iota(jnp.int32, (T * 8, cells), 1)
    owner = lax.rem(t - r_i // 8 + T, T)
    pick = jnp.logical_and(r_i % 8 == q_i // W, owner == (q_i % W) // wt).astype(f32)
    spread = dot(cg_all, pick, 0, 0, highest)
    l_i = lax.broadcasted_iota(jnp.int32, (128, cells), 0)
    w_i = lax.broadcasted_iota(jnp.int32, (128, cells), 1) % W
    spread = jnp.where(jnp.logical_and(l_i // L == w_i % wt, l_i < TILE), spread, 0.0)
    j_i = lax.broadcasted_iota(jnp.int32, (8, 128), 0)
    m_i = lax.broadcasted_iota(jnp.int32, (8, 128), 1)
    fold = jnp.logical_and(m_i % L == j_i, m_i < TILE).astype(f32)
    code = dot(fold, spread, 1, 0, highest)

    latent = dot(proj_t, pooled, 1, 1, highest)
    squashed = jnp.tanh(latent)
    half_j = per_level(levels, lax.broadcasted_iota(jnp.int32, (8, cells), 0), L)
    step = (
        (code / half_j + 2.0 * commit_weight * offset_scale * squashed)
        * offset_scale
        * (1.0 - squashed * squashed)
        * scale
    )
    proj_part = dot(step, pooled, 1, 0, highest)
    pg_t = dot(pscr[:, 0:8], step, 1, 0, highest) * 0.25

    lane = lax.broadcasted_iota(jnp.int32, (C, W), 1)
    bias_sum = jnp.zeros((C, W), f32)
    for f in range(F):
        for h in range(R):
            g = pg_t[:, h * W : (h + 1) * W] * slope_t[f * R + h]
            bias_sum = bias_sum + g
            q0 = (f * R + h) * W
            gt[0:C, q0 : q0 + W] = jnp.where(lane == W - 1, 0.0, pltpu.roll(g, W - 1, 1)).astype(bf16)
            gt[C : 2 * C, q0 : q0 + W] = g.astype(bf16)
            gt[2 * C :, q0 : q0 + W] = jnp.where(lane == 0, 0.0, pltpu.roll(g, 1, 1)).astype(bf16)
    bias_part = dot(jnp.ones((8, W), f32), bias_sum, 1, 1, highest)
    sm_send[...] = jnp.where(lax.broadcasted_iota(jnp.int32, (8, C), 0) == L, bias_part, proj_part)

    def small_space(d):
        return remote(sm_send, sm_recv.at[d], ss_s.at[d], ss_r.at[d], t, lax.rem(s + d, S))

    def small_time(d):
        return remote(st_send, st_recv.at[d], ts_s.at[d], ts_r.at[d], lax.rem(t + d, T), s)

    for d in range(1, S):
        small_space(d).start()

    def core_copy(a):
        return remote(stage1.at[a, 1 - core], recv1.at[a], core_s.at[a], core_r.at[a], t, s + 1 - 2 * core)

    def y_copy(a, d):
        to = lax.rem(y + d, Y)
        return remote(stage2.at[a, to], recv2.at[a, d], y_s.at[a, d], y_r.at[a, d], t, to * 2 + core)

    def tm_copy(to, slot):
        return remote(stage3.at[to], recv3.at[slot], tm_s.at[to], tm_r.at[slot], to, s)

    def products(a):
        rhs = jnp.concatenate(
            [xb[a : a + F, b : b + R].reshape(F * cells, C) for b in range(3)], 1
        )
        res = dot(gt[...], rhs, 1, 0)
        for b in range(3):
            for c in range(3):
                k0 = (b * 3 + c) * C
                for sp in range(S):
                    blk = res[c * C + sp * oc : c * C + (sp + 1) * oc, b * C : (b + 1) * C]
                    acc[a, sp % 2, sp // 2, :, k0 : k0 + C] = blk
                    stage1[a, sp % 2, sp // 2, :, k0 : k0 + C] = blk.astype(bf16)
        core_copy(a).start()

    def fold_core(a):
        core_copy(a).wait_recv()
        for yy in range(Y):
            v = acc[a, core, yy] + recv1[a, yy].astype(f32)
            sum2[a, yy] = v
            stage2[a, yy] = v.astype(bf16)
        for d in range(1, Y):
            y_copy(a, d).start()

    done = [0]

    def fold_y(a):
        v = sum2[a, y]
        for d in range(1, Y):
            y_copy(a, d).wait_recv()
            v = v + recv2[a, d].astype(f32)
        total[:, a * KA : (a + 1) * KA] = v
        while (done[0] + 1) * KT <= (a + 1) * KA:
            to = done[0]
            off = to * KT
            base = off // 128 * 128
            win = total[:, base : base + KTP + 128]
            if off > base:
                win = pltpu.roll(win, KTP + 128 - (off - base), 1)
            win = win[:, 0:KTP]
            own3[to] = win
            stage3[to] = win.astype(bf16)
            start_if(t != to, tm_copy(to, t))
            done[0] += 1

    total[:, KC:] = jnp.zeros((oc, total.shape[1] - KC), f32)
    products(0)
    sm = sm_send[...]
    for d in range(1, S):
        small_space(d).wait_recv()
        sm = sm + sm_recv[d]
    st_send[...] = sm
    for d in range(1, T):
        small_time(d).start()
    products(1)
    fold_core(0)
    products(2)
    fold_core(1)
    fold_y(0)
    fold_core(2)
    fold_y(1)
    fold_y(2)

    for d in range(1, T):
        small_time(d).wait_recv()
        sm = sm + st_recv[d]
    small_out[...] = sm

    res = own3[t]
    for d in range(1, T):
        src = lax.rem(t + d, T)
        tm_copy(src, src).wait_recv()
        res = res + recv3[src].astype(f32)
    weight_out[...] = res

    for sends, _, copy in halos:
        sent_if(sends, copy)
    for d in range(1, T):
        cg_copy(d).wait_send()
        small_time(d).wait_send()
    for d in range(1, S):
        small_space(d).wait_send()
    for a in range(3):
        core_copy(a).wait_send()
        for d in range(1, Y):
            y_copy(a, d).wait_send()
    for to in range(T):
        sent_if(t != to, tm_copy(to, t))


def on_device(T, S, frames, conv_weight, conv_bias, projection, levels, centres, code_grad):
    F, R, W, C = frames.shape
    KC = conv_weight.shape[0]
    KT = KC // T
    KTP = -(-KT // 128) * 128
    oc, Y, cells = C // S, S // 2, R * W
    scale = float(F * T * R * S * W) ** -0.5
    vmem = pl.BlockSpec(memory_space=pltpu.VMEM)
    dma = pltpu.SemaphoreType.DMA
    KA = KC // 3
    quantized, wg, small = pl.pallas_call(
        functools.partial(block_kernel, T, S, scale),
        out_shape=(
            jax.ShapeDtypeStruct(centres.shape, f32),
            jax.ShapeDtypeStruct((oc, KTP), f32),
            jax.ShapeDtypeStruct((8, C), f32),
        ),
        in_specs=[
            pl.BlockSpec(memory_space=pl.ANY), vmem, vmem, vmem,
            pl.BlockSpec(memory_space=pltpu.SMEM), vmem, vmem,
        ],
        out_specs=(vmem, vmem, vmem),
        scratch_shapes=[
            pltpu.VMEM((F + 2, R + 2, W, C), bf16),
            pltpu.VMEM((T, 8, 128), f32),
            pltpu.VMEM((T, 8, 128), f32),
            pltpu.VMEM((C, C), f32),
            pltpu.VMEM((F * R, C, W), f32),
            pltpu.VMEM((3 * C, F * cells), bf16),
            pltpu.VMEM((3, 2, Y, oc, KA), f32),
            pltpu.VMEM((3, 2, Y, oc, KA), bf16),
            pltpu.VMEM((3, Y, oc, KA), bf16),
            pltpu.VMEM((3, Y, oc, KA), f32),
            pltpu.VMEM((3, Y, oc, KA), bf16),
            pltpu.VMEM((3, Y, oc, KA), bf16),
            pltpu.VMEM((oc, KC + KTP + 128), f32),
            pltpu.VMEM((T, oc, KTP), f32),
            pltpu.VMEM((T, oc, KTP), bf16),
            pltpu.VMEM((T, oc, KTP), bf16),
            pltpu.VMEM((8, C), f32),
            pltpu.VMEM((S, 8, C), f32),
            pltpu.VMEM((8, C), f32),
            pltpu.VMEM((T, 8, C), f32),
            dma((3,)), dma((5,)), dma((5,)), dma((T,)), dma((T,)),
            dma((S,)), dma((S,)), dma((T,)), dma((T,)),
            dma((3,)), dma((3,)), dma((3, Y)), dma((3, Y)), dma((T,)), dma((T,)),
        ],
        compiler_params=pltpu.CompilerParams(
            collective_id=0, has_side_effects=True, vmem_limit_bytes=56 * 1024 * 1024
        ),
    )(frames, conv_weight, conv_bias.reshape(1, C), projection, levels, centres, code_grad)
    latent_count = levels.shape[0]
    return quantized, wg[:, :KT].T, small[:latent_count].T, small[latent_count]


def solution(mesh):
    return jax.shard_map(
        functools.partial(on_device, mesh.shape["tm"], mesh.shape["space"]),
        mesh=mesh,
        in_specs=(
            P("tm", "space", None, None),
            P(),
            P(),
            P(),
            P(),
            P(None, "space", "tm"),
            P(None, "space", "tm"),
        ),
        out_specs=(P(None, "space", "tm"), P("tm", "space"), P(), P()),
        check_vma=False,
    )
```

```python
import functools

import jax
import jax.numpy as jnp
from jax import lax
from jax.experimental import pallas as pl
from jax.experimental.pallas import tpu as pltpu
from jax.sharding import PartitionSpec as P

offset_scale = 0.45
commit_weight = 0.25
highest = lax.Precision.HIGHEST
MESH = pl.DeviceIdType.MESH
f32, bf16 = jnp.float32, jnp.bfloat16
core_type, row_type, time_type = f32, bf16, bf16


def dot(a, b, ca, cb, precision=None):
    return lax.dot_general(
        a, b, (((ca,), (cb,)), ((), ())), preferred_element_type=f32, precision=precision
    )


def per_level(levels_ref, index, count):
    half = jnp.ones(index.shape, f32)
    for j in range(count):
        half = jnp.where(index == j, (levels_ref[j].astype(f32) - 1.0) * 0.5, half)
    return half


def block_kernel(
    T, S, scale,
    frames, weight, bias, proj, levels, centres, code_grad,
    quant_out, weight_out, proj_out, bias_out,
    xb, cg_send, cg_recv, pscr, slope_t, gt, acc, stage1, recv1, sum2, stage2, recv2,
    total, own3, stage3, recv3, sm_send, sm_recv, st_send, st_recv,
    local_sem, halo_s, halo_r, cg_s, cg_r, ss_s, ss_r, ts_s, ts_r,
    core_s, core_r, y_s, y_r, tm_s, tm_r,
):
    Y = S // 2
    F, R, W, C = frames.shape
    L = levels.shape[0]
    TILE = code_grad.shape[2]
    oc = C // S
    KC = weight.shape[0]
    KA = KC // 3
    KT = KC // T
    KTP = stage3.shape[2]
    cells = R * W
    t = lax.axis_index("tm")
    s = lax.axis_index("space")
    y, core = s // 2, s % 2
    up_t, dn_t, up_s, dn_s = t < T - 1, t > 0, s < S - 1, s > 0

    barrier = pltpu.get_barrier_semaphore()

    def signal(tt, ss):
        pl.semaphore_signal(barrier, inc=1, device_id=(tt, ss), device_id_type=MESH)

    for d in range(1, S):
        signal(t, lax.rem(s + d, S))
    for d in range(1, T):
        signal(lax.rem(t + d, T), s)
    for ct, dt in ((up_t, 1), (dn_t, -1)):
        for cs_, ds in ((up_s, 1), (dn_s, -1)):
            @pl.when(jnp.logical_and(ct, cs_))
            def _():
                signal(t + dt, s + ds)

    own = pltpu.make_async_copy(frames, xb.at[2 : 2 + F, 1 : 1 + R], local_sem.at[0])
    own.start()
    first = [
        pltpu.make_async_copy(frames.at[0], xb.at[k, 1 : 1 + R], local_sem.at[1 + k])
        for k in range(2)
    ]

    @pl.when(t == 0)
    def _():
        for copy in first:
            copy.start()

    cg_send[...] = jnp.zeros_like(cg_send)
    cg_send[:, 0:R, 0:TILE] = code_grad[...]

    n_t = jnp.where(up_t, 1, 0) + jnp.where(dn_t, 1, 0)
    n_s = jnp.where(up_s, 1, 0) + jnp.where(dn_s, 1, 0)
    pl.semaphore_wait(barrier, (S - 1) + (T - 1) + n_t * n_s)

    def remote(src, dst, ss_, rs_, tt, sp):
        return pltpu.make_async_remote_copy(
            src_ref=src, dst_ref=dst, send_sem=ss_, recv_sem=rs_,
            device_id=(tt, sp), device_id_type=MESH,
        )

    H = R + 1
    halos = [
        (up_s, dn_s, remote(frames.at[:, R - 1], xb.at[2 : 2 + F, 0],
                            halo_s.at[0], halo_r.at[0], t, s + 1)),
        (dn_s, up_s, remote(frames.at[:, 0], xb.at[2 : 2 + F, H],
                            halo_s.at[1], halo_r.at[1], t, s - 1)),
        (up_t, dn_t, remote(frames.at[F - 2 : F], xb.at[0:2, 1:H],
                            halo_s.at[2], halo_r.at[2], t + 1, s)),
        (jnp.logical_and(up_t, up_s), jnp.logical_and(dn_t, dn_s),
         remote(frames.at[F - 2 : F, R - 1], xb.at[0:2, 0],
                halo_s.at[3], halo_r.at[3], t + 1, s + 1)),
        (jnp.logical_and(up_t, dn_s), jnp.logical_and(dn_t, up_s),
         remote(frames.at[F - 2 : F, 0], xb.at[0:2, H],
                halo_s.at[4], halo_r.at[4], t + 1, s - 1)),
    ]

    def start_if(cond, copy):
        @pl.when(cond)
        def _():
            copy.start()

    def recv_if(cond, copy):
        @pl.when(cond)
        def _():
            copy.wait_recv()

    def sent_if(cond, copy):
        @pl.when(cond)
        def _():
            copy.wait_send()

    for sends, _, copy in halos:
        start_if(sends, copy)

    def cg_copy(d):
        to = lax.rem(t + d, T)
        return remote(cg_send.at[to], cg_recv.at[d], cg_s.at[d], cg_r.at[d], to, s)

    for d in range(1, T):
        cg_copy(d).start()

    lane3 = lax.broadcasted_iota(jnp.int32, centres.shape, 2)
    half3 = per_level(levels, lax.rem(lane3, L), L)
    quant_out[...] = (centres[...].astype(f32) - half3) / half3

    pscr[...] = jnp.zeros_like(pscr)
    pscr[0:L] = proj[...]
    proj_t = pscr[...]

    @pl.when(s == 0)
    def _():
        xb[:, 0] = jnp.zeros((F + 2, W, C), bf16)

    @pl.when(s == S - 1)
    def _():
        xb[:, H] = jnp.zeros((F + 2, W, C), bf16)

    row = lax.broadcasted_iota(jnp.int32, (cells, C), 0) % W

    def conv_frame(f):
        slabs = []
        weights = []
        for a in range(3):
            for b in range(3):
                slabs.append(xb[f + a, b : b + R].reshape(cells, C))
                k0 = (a * 3 + b) * 3 * C
                weights.append(
                    jnp.concatenate([weight[k0 + c * C : k0 + (c + 1) * C] for c in range(3)], 1)
                )
        out = dot(jnp.concatenate(slabs, 1), jnp.concatenate(weights, 0), 1, 0)
        left = jnp.where(row == 0, 0.0, pltpu.roll(out[:, 0:C], 1, 0))
        right = jnp.where(row == W - 1, 0.0, pltpu.roll(out[:, 2 * C :], cells - 1, 0))
        pre = out[:, C : 2 * C] + bias[...] + left + right
        sig = 1.0 / (1.0 + jnp.exp(-pre))
        act = (pre * sig).astype(bf16).astype(f32)
        slope = sig * (1.0 + pre * (1.0 - sig))
        for h in range(R):
            slope_t[f * R + h] = slope[h * W : (h + 1) * W].T
        return act

    own.wait()
    for _, gets, copy in halos[:2]:
        recv_if(gets, copy)
    pooled = conv_frame(2) + conv_frame(3)

    for _, gets, copy in halos[2:]:
        recv_if(gets, copy)

    @pl.when(t == 0)
    def _():
        for k in range(2):
            first[k].wait()
            xb[k, 0] = xb[2, 0]
            xb[k, H] = xb[2, H]

    pooled = (pooled + conv_frame(0) + conv_frame(1)) * 0.25

    for d in range(1, T):
        cg_copy(d).wait_recv()
    wt = TILE // L
    mine = cg_send[pl.ds(t, 1)]
    pieces = [mine]
    for d in range(1, T):
        pieces.append(cg_recv[d : d + 1])
    cg_all = jnp.concatenate(pieces, 0).reshape(T * 8, 128)
    r_i = lax.broadcasted_iota(jnp.int32, (T * 8, cells), 0)
    q_i = lax.broadcasted_iota(jnp.int32, (T * 8, cells), 1)
    owner = lax.rem(t - r_i // 8 + T, T)
    pick = jnp.logical_and(r_i % 8 == q_i // W, owner == (q_i % W) // wt).astype(f32)
    spread = dot(cg_all, pick, 0, 0, highest)
    l_i = lax.broadcasted_iota(jnp.int32, (128, cells), 0)
    w_i = lax.broadcasted_iota(jnp.int32, (128, cells), 1) % W
    spread = jnp.where(jnp.logical_and(l_i // L == w_i % wt, l_i < TILE), spread, 0.0)
    j_i = lax.broadcasted_iota(jnp.int32, (8, 128), 0)
    m_i = lax.broadcasted_iota(jnp.int32, (8, 128), 1)
    fold = jnp.logical_and(m_i % L == j_i, m_i < TILE).astype(f32)
    code = dot(fold, spread, 1, 0, highest)

    latent = dot(proj_t, pooled, 1, 1, highest)
    squashed = jnp.tanh(latent)
    half_j = per_level(levels, lax.broadcasted_iota(jnp.int32, (8, cells), 0), L)
    step = (
        (code / half_j + 2.0 * commit_weight * offset_scale * squashed)
        * offset_scale
        * (1.0 - squashed * squashed)
        * scale
    )
    proj_part = dot(step, pooled, 1, 0, highest)
    pg_t = dot(proj_t, step, 0, 0, highest) * 0.25

    lane = lax.broadcasted_iota(jnp.int32, (C, W), 1)
    bias_sum = jnp.zeros((C, W), f32)
    for f in range(F):
        for h in range(R):
            g = pg_t[:, h * W : (h + 1) * W] * slope_t[f * R + h]
            bias_sum = bias_sum + g
            q0 = (f * R + h) * W
            gt[0:C, q0 : q0 + W] = jnp.where(lane == W - 1, 0.0, pltpu.roll(g, W - 1, 1)).astype(bf16)
            gt[C : 2 * C, q0 : q0 + W] = g.astype(bf16)
            gt[2 * C :, q0 : q0 + W] = jnp.where(lane == 0, 0.0, pltpu.roll(g, 1, 1)).astype(bf16)
    bias_part = dot(jnp.ones((8, W), f32), bias_sum, 1, 1, highest)
    sm_send[...] = jnp.where(lax.broadcasted_iota(jnp.int32, (8, C), 0) == L, bias_part, proj_part)

    def small_space(d):
        return remote(sm_send, sm_recv.at[d], ss_s.at[d], ss_r.at[d], t, lax.rem(s + d, S))

    def small_time(d):
        return remote(st_send, st_recv.at[d], ts_s.at[d], ts_r.at[d], lax.rem(t + d, T), s)

    for d in range(1, S):
        small_space(d).start()

    def core_copy(a):
        return remote(stage1.at[a, 1 - core], recv1.at[a], core_s.at[a], core_r.at[a], t, s + 1 - 2 * core)

    def y_copy(a, d):
        to = lax.rem(y + d, Y)
        return remote(stage2.at[a, to], recv2.at[a, d], y_s.at[a, d], y_r.at[a, d], t, to * 2 + core)

    def tm_copy(to, slot):
        return remote(stage3.at[to], recv3.at[slot], tm_s.at[to], tm_r.at[slot], to, s)

    def products(a):
        rhs = jnp.concatenate(
            [xb[a : a + F, b : b + R].reshape(F * cells, C) for b in range(3)], 1
        )
        res = dot(gt[...], rhs, 1, 0)
        for b in range(3):
            for c in range(3):
                k0 = (b * 3 + c) * C
                for sp in range(S):
                    blk = res[c * C + sp * oc : c * C + (sp + 1) * oc, b * C : (b + 1) * C]
                    acc[a, sp % 2, sp // 2, :, k0 : k0 + C] = blk
                    stage1[a, sp % 2, sp // 2, :, k0 : k0 + C] = blk.astype(core_type)
        core_copy(a).start()

    def fold_core(a):
        core_copy(a).wait_recv()
        for yy in range(Y):
            v = acc[a, core, yy] + recv1[a, yy].astype(f32)
            sum2[a, yy] = v
            stage2[a, yy] = v.astype(row_type)
        for d in range(1, Y):
            y_copy(a, d).start()

    done = [0]

    def fold_y(a):
        v = sum2[a, y]
        for d in range(1, Y):
            y_copy(a, d).wait_recv()
            v = v + recv2[a, d].astype(f32)
        total[:, a * KA : (a + 1) * KA] = v
        while (done[0] + 1) * KT <= (a + 1) * KA:
            to = done[0]
            off = to * KT
            base = off // 128 * 128
            win = total[:, base : base + KTP + 128]
            if off > base:
                win = pltpu.roll(win, KTP + 128 - (off - base), 1)
            win = win[:, 0:KTP]
            own3[to] = win
            stage3[to] = win.astype(time_type)
            start_if(t != to, tm_copy(to, t))
            done[0] += 1

    total[:, KC:] = jnp.zeros((oc, total.shape[1] - KC), f32)
    products(0)
    sm = sm_send[...]
    for d in range(1, S):
        small_space(d).wait_recv()
        sm = sm + sm_recv[d]
    st_send[...] = sm
    for d in range(1, T):
        small_time(d).start()
    products(1)
    fold_core(0)
    products(2)
    fold_core(1)
    fold_y(0)
    fold_core(2)
    fold_y(1)
    fold_y(2)

    for d in range(1, T):
        small_time(d).wait_recv()
        sm = sm + st_recv[d]
    proj_out[...] = sm[0:L]
    bias_out[...] = sm[L : L + 1]

    res = own3[t]
    for d in range(1, T):
        src = lax.rem(t + d, T)
        tm_copy(src, src).wait_recv()
        res = res + recv3[src].astype(f32)
    weight_out[...] = res[:, 0:KT]

    for sends, _, copy in halos:
        sent_if(sends, copy)
    for d in range(1, T):
        cg_copy(d).wait_send()
        small_time(d).wait_send()
    for d in range(1, S):
        small_space(d).wait_send()
    for a in range(3):
        core_copy(a).wait_send()
        for d in range(1, Y):
            y_copy(a, d).wait_send()
    for to in range(T):
        sent_if(t != to, tm_copy(to, t))


def on_device(T, S, frames, conv_weight, conv_bias, projection, levels, centres, code_grad):
    F, R, W, C = frames.shape
    KC = conv_weight.shape[0]
    KT = KC // T
    KTP = -(-KT // 128) * 128
    oc, Y, cells = C // S, S // 2, R * W
    scale = float(F * T * R * S * W) ** -0.5
    vmem = pl.BlockSpec(memory_space=pltpu.VMEM)
    dma = pltpu.SemaphoreType.DMA
    KA = KC // 3
    quantized, wg, proj_grad, bias_grad = pl.pallas_call(
        functools.partial(block_kernel, T, S, scale),
        out_shape=(
            jax.ShapeDtypeStruct(centres.shape, f32),
            jax.ShapeDtypeStruct((oc, KT), f32),
            jax.ShapeDtypeStruct((levels.shape[0], C), f32),
            jax.ShapeDtypeStruct((1, C), f32),
        ),
        in_specs=[
            pl.BlockSpec(memory_space=pl.ANY), vmem, vmem, vmem,
            pl.BlockSpec(memory_space=pltpu.SMEM), vmem, vmem,
        ],
        out_specs=(vmem,) * 4,
        scratch_shapes=[
            pltpu.VMEM((F + 2, R + 2, W, C), bf16),
            pltpu.VMEM((T, 8, 128), f32),
            pltpu.VMEM((T, 8, 128), f32),
            pltpu.VMEM((8, C), f32),
            pltpu.VMEM((F * R, C, W), f32),
            pltpu.VMEM((3 * C, F * cells), bf16),
            pltpu.VMEM((3, 2, Y, oc, KA), f32),
            pltpu.VMEM((3, 2, Y, oc, KA), core_type),
            pltpu.VMEM((3, Y, oc, KA), core_type),
            pltpu.VMEM((3, Y, oc, KA), f32),
            pltpu.VMEM((3, Y, oc, KA), row_type),
            pltpu.VMEM((3, Y, oc, KA), row_type),
            pltpu.VMEM((oc, KC + KTP + 128), f32),
            pltpu.VMEM((T, oc, KTP), f32),
            pltpu.VMEM((T, oc, KTP), time_type),
            pltpu.VMEM((T, oc, KTP), time_type),
            pltpu.VMEM((8, C), f32),
            pltpu.VMEM((S, 8, C), f32),
            pltpu.VMEM((8, C), f32),
            pltpu.VMEM((T, 8, C), f32),
            dma((3,)), dma((5,)), dma((5,)), dma((T,)), dma((T,)),
            dma((S,)), dma((S,)), dma((T,)), dma((T,)),
            dma((3,)), dma((3,)), dma((3, Y)), dma((3, Y)), dma((T,)), dma((T,)),
        ],
        compiler_params=pltpu.CompilerParams(
            collective_id=0, has_side_effects=True, vmem_limit_bytes=56 * 1024 * 1024
        ),
    )(frames, conv_weight, conv_bias.reshape(1, C), projection.T, levels, centres, code_grad)
    return quantized, wg.T, proj_grad.T, bias_grad.reshape(C)


def solution(mesh):
    return jax.shard_map(
        functools.partial(on_device, mesh.shape["tm"], mesh.shape["space"]),
        mesh=mesh,
        in_specs=(
            P("tm", "space", None, None),
            P(),
            P(),
            P(),
            P(),
            P(None, "space", "tm"),
            P(None, "space", "tm"),
        ),
        out_specs=(P(None, "space", "tm"), P("tm", "space"), P(), P()),
        check_vma=False,
    )
```

```python
import functools

import jax
import jax.numpy as jnp
from jax import lax
from jax.experimental import pallas as pl
from jax.experimental.pallas import tpu as pltpu
from jax.sharding import PartitionSpec as P

offset_scale = 0.45
commit_weight = 0.25
highest = lax.Precision.HIGHEST
MESH = pl.DeviceIdType.MESH
f32, bf16 = jnp.float32, jnp.bfloat16
core_type, row_type, time_type = f32, bf16, bf16


def dot(a, b, ca, cb, precision=None):
    return lax.dot_general(
        a, b, (((ca,), (cb,)), ((), ())), preferred_element_type=f32, precision=precision
    )


def per_level(levels_ref, index, count):
    half = jnp.ones(index.shape, f32)
    for j in range(count):
        half = jnp.where(index == j, (levels_ref[j].astype(f32) - 1.0) * 0.5, half)
    return half


def block_kernel(
    T, S, scale,
    frames, weight, bias, proj, levels, centres, code_grad,
    quant_out, weight_out, proj_out, bias_out,
    xb, cg_send, cg_recv, pscr, slope_t, gt, acc, stage1, recv1, sum2, stage2, recv2,
    total, own3, stage3, recv3, sm_send, sm_recv, st_send, st_recv,
    local_sem, halo_s, halo_r, corner_s, corner_r, cg_s, cg_r, ss_s, ss_r, ts_s, ts_r,
    core_s, core_r, y_s, y_r, tm_s, tm_r,
):
    Y = S // 2
    F, R, W, C = frames.shape
    L = levels.shape[0]
    TILE = code_grad.shape[2]
    oc = C // S
    KC = weight.shape[0]
    KA = KC // 3
    KT = KC // T
    KTP = stage3.shape[2]
    cells = R * W
    t = lax.axis_index("tm")
    s = lax.axis_index("space")
    y, core = s // 2, s % 2
    up_t, dn_t, up_s, dn_s = t < T - 1, t > 0, s < S - 1, s > 0

    barrier = pltpu.get_barrier_semaphore()

    def signal(tt, ss):
        pl.semaphore_signal(barrier, inc=1, device_id=(tt, ss), device_id_type=MESH)

    for d in range(1, S):
        signal(t, lax.rem(s + d, S))
    for d in range(1, T):
        signal(lax.rem(t + d, T), s)
    own = pltpu.make_async_copy(frames, xb.at[2 : 2 + F, 1 : 1 + R], local_sem.at[0])
    own.start()
    first = [
        pltpu.make_async_copy(frames.at[0], xb.at[k, 1 : 1 + R], local_sem.at[1 + k])
        for k in range(2)
    ]

    @pl.when(t == 0)
    def _():
        for copy in first:
            copy.start()

    cg_send[...] = jnp.zeros_like(cg_send)
    cg_send[:, 0:R, 0:TILE] = code_grad[...]

    pl.semaphore_wait(barrier, (S - 1) + (T - 1))

    def remote(src, dst, ss_, rs_, tt, sp):
        return pltpu.make_async_remote_copy(
            src_ref=src, dst_ref=dst, send_sem=ss_, recv_sem=rs_,
            device_id=(tt, sp), device_id_type=MESH,
        )

    H = R + 1
    halos = [
        (up_s, dn_s, remote(frames.at[:, R - 1], xb.at[2 : 2 + F, 0],
                            halo_s.at[0], halo_r.at[0], t, s + 1)),
        (dn_s, up_s, remote(frames.at[:, 0], xb.at[2 : 2 + F, H],
                            halo_s.at[1], halo_r.at[1], t, s - 1)),
        (up_t, dn_t, remote(frames.at[F - 1], xb.at[1, 1:H],
                            halo_s.at[2], halo_r.at[2], t + 1, s)),
        (up_t, dn_t, remote(frames.at[F - 2], xb.at[0, 1:H],
                            halo_s.at[3], halo_r.at[3], t + 1, s)),
    ]

    def start_if(cond, copy):
        @pl.when(cond)
        def _():
            copy.start()

    def recv_if(cond, copy):
        @pl.when(cond)
        def _():
            copy.wait_recv()

    def sent_if(cond, copy):
        @pl.when(cond)
        def _():
            copy.wait_send()

    for sends, _, copy in halos:
        start_if(sends, copy)

    corners = [
        [
            (jnp.logical_and(dn_t, up_s), jnp.logical_and(dn_t, dn_s),
             remote(xb.at[k, R], xb.at[k, 0], corner_s.at[2 * k], corner_r.at[2 * k], t, s + 1)),
            (jnp.logical_and(dn_t, dn_s), jnp.logical_and(dn_t, up_s),
             remote(xb.at[k, 1], xb.at[k, H], corner_s.at[2 * k + 1], corner_r.at[2 * k + 1], t, s - 1)),
        ]
        for k in range(2)
    ]

    def pass_corners(k):
        _, gets, copy = halos[3 - k]
        recv_if(gets, copy)
        for sends, _, corner in corners[k]:
            start_if(sends, corner)

    def cg_copy(d):
        to = lax.rem(t + d, T)
        return remote(cg_send.at[to], cg_recv.at[d], cg_s.at[d], cg_r.at[d], to, s)

    for d in range(1, T):
        cg_copy(d).start()

    lane3 = lax.broadcasted_iota(jnp.int32, centres.shape, 2)
    half3 = per_level(levels, lax.rem(lane3, L), L)
    quant_out[...] = (centres[...].astype(f32) - half3) / half3

    pscr[...] = jnp.zeros_like(pscr)
    pscr[0:L] = proj[...]
    proj_t = pscr[...]

    @pl.when(s == 0)
    def _():
        xb[:, 0] = jnp.zeros((F + 2, W, C), bf16)

    @pl.when(s == S - 1)
    def _():
        xb[:, H] = jnp.zeros((F + 2, W, C), bf16)

    row = lax.broadcasted_iota(jnp.int32, (cells, C), 0) % W

    def conv_frame(f):
        slabs = []
        weights = []
        for a in range(3):
            for b in range(3):
                slabs.append(xb[f + a, b : b + R].reshape(cells, C))
                k0 = (a * 3 + b) * 3 * C
                weights.append(
                    jnp.concatenate([weight[k0 + c * C : k0 + (c + 1) * C] for c in range(3)], 1)
                )
        out = dot(jnp.concatenate(slabs, 1), jnp.concatenate(weights, 0), 1, 0)
        left = jnp.where(row == 0, 0.0, pltpu.roll(out[:, 0:C], 1, 0))
        right = jnp.where(row == W - 1, 0.0, pltpu.roll(out[:, 2 * C :], cells - 1, 0))
        pre = out[:, C : 2 * C] + bias[...] + left + right
        sig = 1.0 / (1.0 + jnp.exp(-pre))
        act = (pre * sig).astype(bf16).astype(f32)
        slope = sig * (1.0 + pre * (1.0 - sig))
        for h in range(R):
            slope_t[f * R + h] = slope[h * W : (h + 1) * W].T
        return act

    own.wait()
    for _, gets, copy in halos[:2]:
        recv_if(gets, copy)
    pooled = conv_frame(2) + conv_frame(3)

    @pl.when(t == 0)
    def _():
        for k in range(2):
            first[k].wait()
            xb[k, 0] = xb[2, 0]
            xb[k, H] = xb[2, H]

    pass_corners(1)
    for _, gets, copy in corners[1]:
        recv_if(gets, copy)
    pooled = pooled + conv_frame(1)
    pass_corners(0)

    for d in range(1, T):
        cg_copy(d).wait_recv()
    wt = TILE // L
    mine = cg_send[pl.ds(t, 1)]
    pieces = [mine]
    for d in range(1, T):
        pieces.append(cg_recv[d : d + 1])
    cg_all = jnp.concatenate(pieces, 0).reshape(T * 8, 128)
    r_i = lax.broadcasted_iota(jnp.int32, (T * 8, cells), 0)
    q_i = lax.broadcasted_iota(jnp.int32, (T * 8, cells), 1)
    owner = lax.rem(t - r_i // 8 + T, T)
    pick = jnp.logical_and(r_i % 8 == q_i // W, owner == (q_i % W) // wt).astype(f32)
    spread = dot(cg_all, pick, 0, 0, highest)
    l_i = lax.broadcasted_iota(jnp.int32, (128, cells), 0)
    w_i = lax.broadcasted_iota(jnp.int32, (128, cells), 1) % W
    spread = jnp.where(jnp.logical_and(l_i // L == w_i % wt, l_i < TILE), spread, 0.0)
    j_i = lax.broadcasted_iota(jnp.int32, (8, 128), 0)
    m_i = lax.broadcasted_iota(jnp.int32, (8, 128), 1)
    fold = jnp.logical_and(m_i % L == j_i, m_i < TILE).astype(f32)
    code = dot(fold, spread, 1, 0, highest)

    for _, gets, copy in corners[0]:
        recv_if(gets, copy)
    pooled = (pooled + conv_frame(0)) * 0.25

    latent = dot(proj_t, pooled, 1, 1, highest)
    squashed = jnp.tanh(latent)
    half_j = per_level(levels, lax.broadcasted_iota(jnp.int32, (8, cells), 0), L)
    step = (
        (code / half_j + 2.0 * commit_weight * offset_scale * squashed)
        * offset_scale
        * (1.0 - squashed * squashed)
        * scale
    )
    proj_part = dot(step, pooled, 1, 0, highest)
    pg_t = dot(proj_t, step, 0, 0, highest) * 0.25

    lane = lax.broadcasted_iota(jnp.int32, (C, W), 1)
    bias_sum = jnp.zeros((C, W), f32)
    for f in range(F):
        for h in range(R):
            g = pg_t[:, h * W : (h + 1) * W] * slope_t[f * R + h]
            bias_sum = bias_sum + g
            q0 = (f * R + h) * W
            gt[0:C, q0 : q0 + W] = jnp.where(lane == W - 1, 0.0, pltpu.roll(g, W - 1, 1)).astype(bf16)
            gt[C : 2 * C, q0 : q0 + W] = g.astype(bf16)
            gt[2 * C :, q0 : q0 + W] = jnp.where(lane == 0, 0.0, pltpu.roll(g, 1, 1)).astype(bf16)
    bias_part = dot(jnp.ones((8, W), f32), bias_sum, 1, 1, highest)
    sm_send[...] = jnp.where(lax.broadcasted_iota(jnp.int32, (8, C), 0) == L, bias_part, proj_part)

    def small_space(d):
        return remote(sm_send, sm_recv.at[d], ss_s.at[d], ss_r.at[d], t, lax.rem(s + d, S))

    def small_time(d):
        return remote(st_send, st_recv.at[d], ts_s.at[d], ts_r.at[d], lax.rem(t + d, T), s)

    for d in range(1, S):
        small_space(d).start()

    def core_copy(a):
        return remote(stage1.at[a, 1 - core], recv1.at[a], core_s.at[a], core_r.at[a], t, s + 1 - 2 * core)

    def y_copy(a, d):
        to = lax.rem(y + d, Y)
        return remote(stage2.at[a, to], recv2.at[a, d], y_s.at[a, d], y_r.at[a, d], t, to * 2 + core)

    def tm_copy(to, slot):
        return remote(stage3.at[to], recv3.at[slot], tm_s.at[to], tm_r.at[slot], to, s)

    def products(a):
        rhs = jnp.concatenate(
            [xb[a : a + F, b : b + R].reshape(F * cells, C) for b in range(3)], 1
        )
        res = dot(gt[...], rhs, 1, 0)
        for b in range(3):
            for c in range(3):
                k0 = (b * 3 + c) * C
                for sp in range(S):
                    blk = res[c * C + sp * oc : c * C + (sp + 1) * oc, b * C : (b + 1) * C]
                    acc[a, sp % 2, sp // 2, :, k0 : k0 + C] = blk
                    stage1[a, sp % 2, sp // 2, :, k0 : k0 + C] = blk.astype(core_type)
        core_copy(a).start()

    def fold_core(a):
        core_copy(a).wait_recv()
        for yy in range(Y):
            v = acc[a, core, yy] + recv1[a, yy].astype(f32)
            sum2[a, yy] = v
            stage2[a, yy] = v.astype(row_type)
        for d in range(1, Y):
            y_copy(a, d).start()

    folded, sent = set(), set()

    def fold_y(a):
        v = sum2[a, y]
        for d in range(1, Y):
            y_copy(a, d).wait_recv()
            v = v + recv2[a, d].astype(f32)
        total[:, a * KA : (a + 1) * KA] = v
        folded.add(a)
        for to in range(T):
            off = to * KT
            if to in sent or not {off // KA, (off + KT - 1) // KA} <= folded:
                continue
            sent.add(to)
            base = off // 128 * 128
            win = total[:, base : base + KTP + 128]
            if off > base:
                win = pltpu.roll(win, KTP + 128 - (off - base), 1)
            win = win[:, 0:KTP]
            own3[to] = win
            stage3[to] = win.astype(time_type)
            start_if(t != to, tm_copy(to, t))

    total[...] = jnp.zeros(total.shape, f32)
    products(0)
    sm = sm_send[...]
    for d in range(1, S):
        small_space(d).wait_recv()
        sm = sm + sm_recv[d]
    st_send[...] = sm
    for d in range(1, T):
        small_time(d).start()
    products(2)
    fold_core(0)
    products(1)
    fold_core(2)
    fold_y(0)
    fold_core(1)
    fold_y(2)
    fold_y(1)

    for d in range(1, T):
        small_time(d).wait_recv()
        sm = sm + st_recv[d]
    proj_out[...] = sm[0:L]
    bias_out[...] = sm[L : L + 1]

    res = own3[t]
    for d in range(1, T):
        src = lax.rem(t + d, T)
        tm_copy(src, src).wait_recv()
        res = res + recv3[src].astype(f32)
    weight_out[...] = res[:, 0:KT]

    for sends, _, copy in halos + corners[0] + corners[1]:
        sent_if(sends, copy)
    for d in range(1, T):
        cg_copy(d).wait_send()
        small_time(d).wait_send()
    for d in range(1, S):
        small_space(d).wait_send()
    for a in range(3):
        core_copy(a).wait_send()
        for d in range(1, Y):
            y_copy(a, d).wait_send()
    for to in range(T):
        sent_if(t != to, tm_copy(to, t))


def on_device(T, S, frames, conv_weight, conv_bias, projection, levels, centres, code_grad):
    F, R, W, C = frames.shape
    KC = conv_weight.shape[0]
    KT = KC // T
    KTP = -(-KT // 128) * 128
    oc, Y, cells = C // S, S // 2, R * W
    scale = float(F * T * R * S * W) ** -0.5
    vmem = pl.BlockSpec(memory_space=pltpu.VMEM)
    dma = pltpu.SemaphoreType.DMA
    KA = KC // 3
    quantized, wg, proj_grad, bias_grad = pl.pallas_call(
        functools.partial(block_kernel, T, S, scale),
        out_shape=(
            jax.ShapeDtypeStruct(centres.shape, f32),
            jax.ShapeDtypeStruct((oc, KT), f32),
            jax.ShapeDtypeStruct((levels.shape[0], C), f32),
            jax.ShapeDtypeStruct((1, C), f32),
        ),
        in_specs=[
            pl.BlockSpec(memory_space=pl.ANY), vmem, vmem, vmem,
            pl.BlockSpec(memory_space=pltpu.SMEM), vmem, vmem,
        ],
        out_specs=(vmem,) * 4,
        scratch_shapes=[
            pltpu.VMEM((F + 2, R + 2, W, C), bf16),
            pltpu.VMEM((T, 8, 128), f32),
            pltpu.VMEM((T, 8, 128), f32),
            pltpu.VMEM((8, C), f32),
            pltpu.VMEM((F * R, C, W), f32),
            pltpu.VMEM((3 * C, F * cells), bf16),
            pltpu.VMEM((3, 2, Y, oc, KA), f32),
            pltpu.VMEM((3, 2, Y, oc, KA), core_type),
            pltpu.VMEM((3, Y, oc, KA), core_type),
            pltpu.VMEM((3, Y, oc, KA), f32),
            pltpu.VMEM((3, Y, oc, KA), row_type),
            pltpu.VMEM((3, Y, oc, KA), row_type),
            pltpu.VMEM((oc, KC + KTP + 128), f32),
            pltpu.VMEM((T, oc, KTP), f32),
            pltpu.VMEM((T, oc, KTP), time_type),
            pltpu.VMEM((T, oc, KTP), time_type),
            pltpu.VMEM((8, C), f32),
            pltpu.VMEM((S, 8, C), f32),
            pltpu.VMEM((8, C), f32),
            pltpu.VMEM((T, 8, C), f32),
            dma((3,)), dma((4,)), dma((4,)), dma((4,)), dma((4,)), dma((T,)), dma((T,)),
            dma((S,)), dma((S,)), dma((T,)), dma((T,)),
            dma((3,)), dma((3,)), dma((3, Y)), dma((3, Y)), dma((T,)), dma((T,)),
        ],
        compiler_params=pltpu.CompilerParams(
            collective_id=0, has_side_effects=True, vmem_limit_bytes=56 * 1024 * 1024
        ),
    )(frames, conv_weight, conv_bias.reshape(1, C), projection.T, levels, centres, code_grad)
    return quantized, wg.T, proj_grad.T, bias_grad.reshape(C)


def solution(mesh):
    return jax.shard_map(
        functools.partial(on_device, mesh.shape["tm"], mesh.shape["space"]),
        mesh=mesh,
        in_specs=(
            P("tm", "space", None, None),
            P(),
            P(),
            P(),
            P(),
            P(None, "space", "tm"),
            P(None, "space", "tm"),
        ),
        out_specs=(P(None, "space", "tm"), P("tm", "space"), P(), P()),
        check_vma=False,
    )
```

```python
import functools

import jax
import jax.numpy as jnp
from jax import lax
from jax.experimental import pallas as pl
from jax.experimental.pallas import tpu as pltpu
from jax.sharding import PartitionSpec as P

offset_scale = 0.45
commit_weight = 0.25
highest = lax.Precision.HIGHEST
MESH = pl.DeviceIdType.MESH
f32, bf16 = jnp.float32, jnp.bfloat16
core_type, row_type, time_type = f32, bf16, bf16


def dot(a, b, ca, cb, precision=None):
    return lax.dot_general(
        a, b, (((ca,), (cb,)), ((), ())), preferred_element_type=f32, precision=precision
    )


def per_level(levels_ref, index, count):
    half = jnp.ones(index.shape, f32)
    for j in range(count):
        half = jnp.where(index == j, (levels_ref[j].astype(f32) - 1.0) * 0.5, half)
    return half


def block_kernel(
    T, S, scale,
    frames, weight, bias, proj, levels, code_grad,
    weight_out, small_out,
    xb, cg_send, cg_recv, pscr, slope_t, gt, acc, stage1, recv1, sum2, stage2, recv2,
    total, own3, stage3, recv3, sm_send, sm_recv, st_send, st_recv,
    local_sem, halo_s, halo_r, cg_s, cg_r, ss_s, ss_r, ts_s, ts_r,
    core_s, core_r, y_s, y_r, tm_s, tm_r,
):
    Y = S // 2
    F, R, W, C = frames.shape
    L = levels.shape[0]
    TILE = code_grad.shape[2]
    oc = C // S
    KC = weight.shape[0]
    KA = KC // 3
    KT = KC // T
    KTP = stage3.shape[2]
    cells = R * W
    t = lax.axis_index("tm")
    s = lax.axis_index("space")
    y, core = s // 2, s % 2
    up_t, dn_t, up_s, dn_s = t < T - 1, t > 0, s < S - 1, s > 0

    barrier = pltpu.get_barrier_semaphore()

    def signal(tt, ss):
        pl.semaphore_signal(barrier, inc=1, device_id=(tt, ss), device_id_type=MESH)

    for d in range(1, S):
        signal(t, lax.rem(s + d, S))
    for d in range(1, T):
        signal(lax.rem(t + d, T), s)
    for ct, dt in ((up_t, 1), (dn_t, -1)):
        for cs_, ds in ((up_s, 1), (dn_s, -1)):
            @pl.when(jnp.logical_and(ct, cs_))
            def _():
                signal(t + dt, s + ds)

    own = pltpu.make_async_copy(frames, xb.at[2 : 2 + F, 1 : 1 + R], local_sem.at[0])
    own.start()
    first = [
        pltpu.make_async_copy(frames.at[0], xb.at[k, 1 : 1 + R], local_sem.at[1 + k])
        for k in range(2)
    ]

    @pl.when(t == 0)
    def _():
        for copy in first:
            copy.start()

    cg_send[...] = jnp.zeros_like(cg_send)
    cg_send[:, 0:R, 0:TILE] = code_grad[...]

    n_t = jnp.where(up_t, 1, 0) + jnp.where(dn_t, 1, 0)
    n_s = jnp.where(up_s, 1, 0) + jnp.where(dn_s, 1, 0)
    pl.semaphore_wait(barrier, (S - 1) + (T - 1) + n_t * n_s)

    def remote(src, dst, ss_, rs_, tt, sp):
        return pltpu.make_async_remote_copy(
            src_ref=src, dst_ref=dst, send_sem=ss_, recv_sem=rs_,
            device_id=(tt, sp), device_id_type=MESH,
        )

    H = R + 1
    halos = [
        (up_s, dn_s, remote(frames.at[:, R - 1], xb.at[2 : 2 + F, 0],
                            halo_s.at[0], halo_r.at[0], t, s + 1)),
        (dn_s, up_s, remote(frames.at[:, 0], xb.at[2 : 2 + F, H],
                            halo_s.at[1], halo_r.at[1], t, s - 1)),
        (up_t, dn_t, remote(frames.at[F - 2 : F], xb.at[0:2, 1:H],
                            halo_s.at[2], halo_r.at[2], t + 1, s)),
        (jnp.logical_and(up_t, up_s), jnp.logical_and(dn_t, dn_s),
         remote(frames.at[F - 2 : F, R - 1], xb.at[0:2, 0],
                halo_s.at[3], halo_r.at[3], t + 1, s + 1)),
        (jnp.logical_and(up_t, dn_s), jnp.logical_and(dn_t, up_s),
         remote(frames.at[F - 2 : F, 0], xb.at[0:2, H],
                halo_s.at[4], halo_r.at[4], t + 1, s - 1)),
    ]

    def start_if(cond, copy):
        @pl.when(cond)
        def _():
            copy.start()

    def recv_if(cond, copy):
        @pl.when(cond)
        def _():
            copy.wait_recv()

    def sent_if(cond, copy):
        @pl.when(cond)
        def _():
            copy.wait_send()

    for sends, _, copy in halos:
        start_if(sends, copy)

    def cg_copy(d):
        to = lax.rem(t + d, T)
        return remote(cg_send.at[to], cg_recv.at[d], cg_s.at[d], cg_r.at[d], to, s)

    for d in range(1, T):
        cg_copy(d).start()

    pscr[...] = jnp.zeros_like(pscr)
    pscr[0:L] = proj[...]
    proj_t = pscr[...]

    @pl.when(s == 0)
    def _():
        xb[:, 0] = jnp.zeros((F + 2, W, C), bf16)

    @pl.when(s == S - 1)
    def _():
        xb[:, H] = jnp.zeros((F + 2, W, C), bf16)

    row = lax.broadcasted_iota(jnp.int32, (cells, C), 0) % W

    def conv_frame(f):
        slabs = []
        weights = []
        for a in range(3):
            for b in range(3):
                slabs.append(xb[f + a, b : b + R].reshape(cells, C))
                k0 = (a * 3 + b) * 3 * C
                weights.append(
                    jnp.concatenate([weight[k0 + c * C : k0 + (c + 1) * C] for c in range(3)], 1)
                )
        out = dot(jnp.concatenate(slabs, 1), jnp.concatenate(weights, 0), 1, 0)
        left = jnp.where(row == 0, 0.0, pltpu.roll(out[:, 0:C], 1, 0))
        right = jnp.where(row == W - 1, 0.0, pltpu.roll(out[:, 2 * C :], cells - 1, 0))
        pre = out[:, C : 2 * C] + bias[...] + left + right
        sig = 1.0 / (1.0 + jnp.exp(-pre))
        act = (pre * sig).astype(bf16).astype(f32)
        slope = sig * (1.0 + pre * (1.0 - sig))
        for h in range(R):
            slope_t[f * R + h] = slope[h * W : (h + 1) * W].T
        return act

    own.wait()
    for _, gets, copy in halos[:2]:
        recv_if(gets, copy)
    pooled = conv_frame(2) + conv_frame(3)

    for _, gets, copy in halos[2:]:
        recv_if(gets, copy)

    @pl.when(t == 0)
    def _():
        for k in range(2):
            first[k].wait()
            xb[k, 0] = xb[2, 0]
            xb[k, H] = xb[2, H]

    pooled = (pooled + conv_frame(0) + conv_frame(1)) * 0.25

    for d in range(1, T):
        cg_copy(d).wait_recv()
    wt = TILE // L
    mine = cg_send[pl.ds(t, 1)]
    pieces = [mine]
    for d in range(1, T):
        pieces.append(cg_recv[d : d + 1])
    cg_all = jnp.concatenate(pieces, 0).reshape(T * 8, 128)
    r_i = lax.broadcasted_iota(jnp.int32, (T * 8, cells), 0)
    q_i = lax.broadcasted_iota(jnp.int32, (T * 8, cells), 1)
    owner = lax.rem(t - r_i // 8 + T, T)
    pick = jnp.logical_and(r_i % 8 == q_i // W, owner == (q_i % W) // wt).astype(f32)
    spread = dot(cg_all, pick, 0, 0, highest)
    l_i = lax.broadcasted_iota(jnp.int32, (128, cells), 0)
    w_i = lax.broadcasted_iota(jnp.int32, (128, cells), 1) % W
    spread = jnp.where(jnp.logical_and(l_i // L == w_i % wt, l_i < TILE), spread, 0.0)
    j_i = lax.broadcasted_iota(jnp.int32, (8, 128), 0)
    m_i = lax.broadcasted_iota(jnp.int32, (8, 128), 1)
    fold = jnp.logical_and(m_i % L == j_i, m_i < TILE).astype(f32)
    code = dot(fold, spread, 1, 0, highest)

    latent = dot(proj_t, pooled, 1, 1, highest)
    squashed = jnp.tanh(latent)
    half_j = per_level(levels, lax.broadcasted_iota(jnp.int32, (8, cells), 0), L)
    step = (
        (code / half_j + 2.0 * commit_weight * offset_scale * squashed)
        * offset_scale
        * (1.0 - squashed * squashed)
        * scale
    )
    proj_part = dot(step, pooled, 1, 0, highest)
    pg_t = dot(proj_t, step, 0, 0, highest) * 0.25

    lane = lax.broadcasted_iota(jnp.int32, (C, W), 1)
    bias_sum = jnp.zeros((C, W), f32)
    for f in range(F):
        for h in range(R):
            g = pg_t[:, h * W : (h + 1) * W] * slope_t[f * R + h]
            bias_sum = bias_sum + g
            q0 = (f * R + h) * W
            gt[0:C, q0 : q0 + W] = jnp.where(lane == W - 1, 0.0, pltpu.roll(g, W - 1, 1)).astype(bf16)
            gt[C : 2 * C, q0 : q0 + W] = g.astype(bf16)
            gt[2 * C :, q0 : q0 + W] = jnp.where(lane == 0, 0.0, pltpu.roll(g, 1, 1)).astype(bf16)
    bias_part = dot(jnp.ones((8, W), f32), bias_sum, 1, 1, highest)
    sm_send[...] = jnp.where(lax.broadcasted_iota(jnp.int32, (8, C), 0) == L, bias_part, proj_part)

    def small_space(d):
        return remote(sm_send, sm_recv.at[d], ss_s.at[d], ss_r.at[d], t, lax.rem(s + d, S))

    def small_time(d):
        return remote(st_send, st_recv.at[d], ts_s.at[d], ts_r.at[d], lax.rem(t + d, T), s)

    for d in range(1, S):
        small_space(d).start()

    def core_copy(a):
        return remote(stage1.at[a, 1 - core], recv1.at[a], core_s.at[a], core_r.at[a], t, s + 1 - 2 * core)

    def y_copy(a, d):
        to = lax.rem(y + d, Y)
        return remote(stage2.at[a, to], recv2.at[a, d], y_s.at[a, d], y_r.at[a, d], t, to * 2 + core)

    def tm_copy(to, slot):
        return remote(stage3.at[to], recv3.at[slot], tm_s.at[to], tm_r.at[slot], to, s)

    def products(a):
        rhs = jnp.concatenate(
            [xb[a : a + F, b : b + R].reshape(F * cells, C) for b in range(3)], 1
        )
        res = dot(gt[...], rhs, 1, 0)
        for b in range(3):
            for c in range(3):
                k0 = (b * 3 + c) * C
                for sp in range(S):
                    blk = res[c * C + sp * oc : c * C + (sp + 1) * oc, b * C : (b + 1) * C]
                    acc[a, sp % 2, sp // 2, :, k0 : k0 + C] = blk
                    stage1[a, sp % 2, sp // 2, :, k0 : k0 + C] = blk.astype(core_type)
        core_copy(a).start()

    def fold_core(a):
        core_copy(a).wait_recv()
        for yy in range(Y):
            v = acc[a, core, yy] + recv1[a, yy].astype(f32)
            sum2[a, yy] = v
            stage2[a, yy] = v.astype(row_type)
        for d in range(1, Y):
            y_copy(a, d).start()

    done = [0]

    def fold_y(a):
        v = sum2[a, y]
        for d in range(1, Y):
            y_copy(a, d).wait_recv()
            v = v + recv2[a, d].astype(f32)
        total[:, a * KA : (a + 1) * KA] = v
        while (done[0] + 1) * KT <= (a + 1) * KA:
            to = done[0]
            off = to * KT
            base = off // 128 * 128
            win = total[:, base : base + KTP + 128]
            if off > base:
                win = pltpu.roll(win, KTP + 128 - (off - base), 1)
            win = win[:, 0:KTP]
            own3[to] = win
            stage3[to] = win.astype(time_type)
            start_if(t != to, tm_copy(to, t))
            done[0] += 1

    total[:, KC:] = jnp.zeros((oc, total.shape[1] - KC), f32)
    products(0)
    sm = sm_send[...]
    for d in range(1, S):
        small_space(d).wait_recv()
        sm = sm + sm_recv[d]
    st_send[...] = sm
    for d in range(1, T):
        small_time(d).start()
    products(1)
    fold_core(0)
    products(2)
    fold_core(1)
    fold_y(0)
    fold_core(2)
    fold_y(1)
    fold_y(2)

    for d in range(1, T):
        small_time(d).wait_recv()
        sm = sm + st_recv[d]
    small_out[...] = sm

    res = own3[t]
    for d in range(1, T):
        src = lax.rem(t + d, T)
        tm_copy(src, src).wait_recv()
        res = res + recv3[src].astype(f32)
    weight_out[...] = res[:, 0:KT]

    for sends, _, copy in halos:
        sent_if(sends, copy)
    for d in range(1, T):
        cg_copy(d).wait_send()
        small_time(d).wait_send()
    for d in range(1, S):
        small_space(d).wait_send()
    for a in range(3):
        core_copy(a).wait_send()
        for d in range(1, Y):
            y_copy(a, d).wait_send()
    for to in range(T):
        sent_if(t != to, tm_copy(to, t))


def finish_kernel(levels, centres, wg, small, quant_out, weight_out, proj_out, bias_out):
    L = levels.shape[0]
    lane = lax.broadcasted_iota(jnp.int32, centres.shape, 2)
    half = per_level(levels, lax.rem(lane, L), L)
    quant_out[...] = (centres[...].astype(f32) - half) / half
    weight_out[...] = wg[...]
    proj_out[...] = small[0:L]
    bias_out[...] = small[L : L + 1]


def on_device(T, S, frames, conv_weight, conv_bias, projection, levels, centres, code_grad):
    F, R, W, C = frames.shape
    KC = conv_weight.shape[0]
    KT = KC // T
    KTP = -(-KT // 128) * 128
    oc, Y, cells = C // S, S // 2, R * W
    scale = float(F * T * R * S * W) ** -0.5
    vmem = pl.BlockSpec(memory_space=pltpu.VMEM)
    dma = pltpu.SemaphoreType.DMA
    KA = KC // 3
    wg, small = pl.pallas_call(
        functools.partial(block_kernel, T, S, scale),
        out_shape=(
            jax.ShapeDtypeStruct((oc, KT), f32),
            jax.ShapeDtypeStruct((8, C), f32),
        ),
        in_specs=[
            pl.BlockSpec(memory_space=pl.ANY), vmem, vmem, vmem,
            pl.BlockSpec(memory_space=pltpu.SMEM), vmem,
        ],
        out_specs=(vmem, vmem),
        scratch_shapes=[
            pltpu.VMEM((F + 2, R + 2, W, C), bf16),
            pltpu.VMEM((T, 8, 128), f32),
            pltpu.VMEM((T, 8, 128), f32),
            pltpu.VMEM((8, C), f32),
            pltpu.VMEM((F * R, C, W), f32),
            pltpu.VMEM((3 * C, F * cells), bf16),
            pltpu.VMEM((3, 2, Y, oc, KA), f32),
            pltpu.VMEM((3, 2, Y, oc, KA), core_type),
            pltpu.VMEM((3, Y, oc, KA), core_type),
            pltpu.VMEM((3, Y, oc, KA), f32),
            pltpu.VMEM((3, Y, oc, KA), row_type),
            pltpu.VMEM((3, Y, oc, KA), row_type),
            pltpu.VMEM((oc, KC + KTP + 128), f32),
            pltpu.VMEM((T, oc, KTP), f32),
            pltpu.VMEM((T, oc, KTP), time_type),
            pltpu.VMEM((T, oc, KTP), time_type),
            pltpu.VMEM((8, C), f32),
            pltpu.VMEM((S, 8, C), f32),
            pltpu.VMEM((8, C), f32),
            pltpu.VMEM((T, 8, C), f32),
            dma((3,)), dma((5,)), dma((5,)), dma((T,)), dma((T,)),
            dma((S,)), dma((S,)), dma((T,)), dma((T,)),
            dma((3,)), dma((3,)), dma((3, Y)), dma((3, Y)), dma((T,)), dma((T,)),
        ],
        compiler_params=pltpu.CompilerParams(
            collective_id=0, has_side_effects=True, vmem_limit_bytes=56 * 1024 * 1024
        ),
    )(frames, conv_weight, conv_bias.reshape(1, C), projection.T, levels, code_grad)
    L = levels.shape[0]
    quantized, wg, proj_grad, bias_grad = pl.pallas_call(
        finish_kernel,
        out_shape=(
            jax.ShapeDtypeStruct(centres.shape, f32),
            jax.ShapeDtypeStruct(wg.shape, f32),
            jax.ShapeDtypeStruct((L, C), f32),
            jax.ShapeDtypeStruct((1, C), f32),
        ),
        in_specs=[pl.BlockSpec(memory_space=pltpu.SMEM), vmem, vmem, vmem],
        out_specs=(vmem,) * 4,
    )(levels, centres, wg, small)
    return quantized, wg.T, proj_grad.T, bias_grad.reshape(C)


def solution(mesh):
    return jax.shard_map(
        functools.partial(on_device, mesh.shape["tm"], mesh.shape["space"]),
        mesh=mesh,
        in_specs=(
            P("tm", "space", None, None),
            P(),
            P(),
            P(),
            P(),
            P(None, "space", "tm"),
            P(None, "space", "tm"),
        ),
        out_specs=(P(None, "space", "tm"), P("tm", "space"), P(), P()),
        check_vma=False,
    )
```
